32 devices in a mesh: groups: 2 (over y), hosts: 4 (over z), mp: 4 (over x, core).
Axes of the slice: x: 2, y: 2, z: 4, core: 2. Of those that a mesh axis runs over, the one named last changes fastest.
Arguments:
- hidden: bfloat16 [256, 4096], P(('groups', 'hosts'), 'mp'), parts along dimension 0, may hold values from -6 to 6
- base_query_projection: bfloat16 [256, 4096], P(('groups', 'hosts'), 'mp'), parts along dimension 0, may hold values from -160 to 160
- base_key_projection: bfloat16 [256, 4096], P(('groups', 'hosts'), 'mp'), parts along dimension 0, may hold values from -6 to 6
- base_value_projection: bfloat16 [256, 4096], P(('groups', 'hosts'), 'mp'), parts along dimension 0, may hold values from -6 to 6
- adapter_input_factors: bfloat16 [8, 4096, 128], P(('groups', 'hosts'), 'mp'), parts along dimension 0, may hold values from -0.09375 to 0.09375
- adapter_output_factors: bfloat16 [8, 2, 64, 4096], P(('groups', 'hosts'), None, None, 'mp'), parts along dimension 0, may hold values from -0.75 to 0.75
- statement_prefix_cache: bfloat16 [32, 2, 128, 4096], P(('groups', 'hosts'), None, None, 'mp'), parts along dimension 0, may hold values from -6 to 6
- generated_token_cache: bfloat16 [256, 2, 8, 4096], P(('groups', 'hosts'), None, None, 'mp'), parts along dimension 0, may hold values from -6 to 6
- attempt_theorem_index: int32 [256], P(('groups', 'hosts')), parts along dimension 0, may hold values from 0 to 3, as said below
- host_live_count: int32 [8], P(('groups', 'hosts')), parts along dimension 0, may hold values from 8 to 32, as said below
- adapter_pool_row: int32 [8], P('groups'), parts along dimension 0, may hold values from 0 to 3, as said below
- prefix_pool_row: int32 [8, 4], P('groups'), parts along dimension 0, may hold values from 0 to 15, as said below
- prefix_block_count: int32 [8], P('groups'), parts along dimension 0, may hold values from 1 to 4
Outputs:
- attended: bfloat16 [256, 4096], P(('groups', 'hosts'), 'mp'), parts along dimension 0
- key_rows: bfloat16 [256, 4096], P(('groups', 'hosts'), 'mp'), parts along dimension 0
- value_rows: bfloat16 [256, 4096], P(('groups', 'hosts'), 'mp'), parts along dimension 0
The draws below stay inside these ranges and needn't reach their ends.
There are 2 independent parts, one for each index of `groups`. The reference program is written for one: setup_inputs(seed, part) draws one part's arguments, and reference() takes and returns one part's arrays. A program takes and returns all parts, laid end to end along the dimension named above; each array names one. Nothing has to cross between parts.
Inputs may be any that keep to these rules, and one draw needn't show every extreme that they name: `attempt_theorem_index`: among the live attempts of one host, at most 8 name theorems whose adapter lies on any one host, and for each block index at most 8 name theorems whose block of that index lies on any one host. One host holds the adapters named by 8 live attempts of every host, and one host holds the first blocks named by 8 live attempts of every host. `host_live_count`: rows at or above a host's count are empty; some host has all 32 rows live. `adapter_pool_row`: all entries differ; pool row p lies on host p. `prefix_pool_row`: all entries differ; pool row p lies on host p // 4.
All inputs are finite; a program needn't handle non-finite values.
Results may differ from the reference program's by a relative error of at most 0.011.
Values may be sent and summed in bfloat16 or wider, within the bound.
No kernel may reach another device: no remote copies, remote signals or barrier semaphores. Data moves between devices by JAX's collectives and lax.ppermute only.
A program may use at most 64 MiB of HBM per device.

```python
import jax
import jax.numpy as jnp
from jax import lax

MODEL_WIDTH = 4096
ATTENTION_HEADS = 32
HEAD_SIZE = 128
ADAPTER_RANK = 64
BLK = 128
PBLK = 4
ATT_DEV = 32
SUFFIX = 8
THM_DEV = 1
HOSTS = 4
ATTEMPTS = 128
THEOREM_VARIANTS = 4
BLK_DEV = 4
BLOCKS = 16


def layout_plan(key):
    streams = jax.random.split(jax.random.fold_in(key, 17), 9)
    adapter_perm = jax.random.permutation(streams[0], THEOREM_VARIANTS).astype(jnp.int32)
    adapter_inverse = jnp.argsort(adapter_perm).astype(jnp.int32)
    owner_of = adapter_perm // THM_DEV
    slot_of = adapter_perm % THM_DEV
    host_perms = jax.vmap(lambda subkey: jax.random.permutation(subkey, HOSTS))(jax.random.split(streams[1], PBLK)).astype(jnp.int32)
    block_table = host_perms[:, owner_of].T * BLK_DEV + jnp.arange(PBLK, dtype=jnp.int32)[None, :] * THM_DEV + slot_of[:, None]
    hottest = jax.random.randint(streams[2], (), 0, HOSTS).astype(jnp.int32)
    orders = jax.vmap(lambda subkey: jax.random.permutation(subkey, HOSTS))(jax.random.split(streams[3], HOSTS)).astype(jnp.int32)
    columns = jnp.arange(HOSTS, dtype=jnp.int32)
    hot_where = jnp.sum(jnp.where(orders == hottest, columns[None, :], 0), axis=1)
    capacity = max(1, ATT_DEV // HOSTS)
    ordinal = jnp.arange(ATT_DEV, dtype=jnp.int32)
    owner_rows = jnp.take_along_axis(orders, ((ordinal // capacity)[None, :] + hot_where[:, None]) % HOSTS, axis=1)
    choose = jax.random.randint(streams[5], (HOSTS, ATT_DEV), 0, THM_DEV).astype(jnp.int32)
    theorems = adapter_inverse[owner_rows * THM_DEV + choose].reshape(ATTEMPTS)
    counts = jax.random.randint(streams[6], (HOSTS,), capacity, ATT_DEV + 1).astype(jnp.int32)
    filled = jax.random.randint(streams[7], (), 0, HOSTS)
    counts = jnp.where(columns == filled, ATT_DEV, counts).astype(jnp.int32)
    lengths = jax.random.randint(streams[8], (THEOREM_VARIANTS,), 1, PBLK + 1).astype(jnp.int32)
    lengths = lengths.at[adapter_inverse[hottest * THM_DEV]].set(PBLK)
    return (theorems, counts, adapter_perm, block_table.astype(jnp.int32), lengths)


def draw_attempt_theorem_index(key, part):
    return layout_plan(key)[0]


def draw_host_live_count(key, part):
    return layout_plan(key)[1]


def draw_adapter_pool_row(key, part):
    return layout_plan(key)[2]


def draw_prefix_pool_row(key, part):
    return layout_plan(key)[3]


def draw_prefix_block_count(key, part):
    return layout_plan(key)[4]


def draw_base_query_projection(key, part):
    shape_rows = (ATTEMPTS, ATTENTION_HEADS * HEAD_SIZE)
    values = jnp.clip(1.8 * jax.random.normal(jax.random.fold_in(key, 3), shape_rows, jnp.float32), -10.0, 10.0)
    return values.astype(jnp.bfloat16)


def shard_levels(stream_key, shape, cuts, smallest, high):
    loudness, own = 1.0, jax.random.fold_in(stream_key, 6)
    for dim, shards_of in cuts:
        heights = jnp.exp(jax.random.uniform(jax.random.fold_in(own, dim), (shards_of,), jnp.float32, smallest / len(cuts), high / len(cuts)))
        loudness = loudness * jnp.repeat(heights, shape[dim] // shards_of).reshape([-1 if axis == dim else 1 for axis in range(len(shape))])
    return loudness


def scatter_about(stream_key, extent, deviation, bound, cuts=(), kind=jnp.bfloat16):
    entries = jax.random.normal(stream_key, extent, jnp.float32) * deviation
    if len(cuts) > 0:
        entries = shard_levels(stream_key, extent, cuts, -0.22, 0.18) * entries
    return jnp.clip(entries, min=-bound, max=bound).astype(kind)


def setup_inputs(seed: int = 0, part: int = 0) -> dict:
    key_list = jax.random.split(jax.random.key(seed), 14)
    part_keys = jax.random.split(jax.random.fold_in(key_list[13], part), 14)
    return {
        "hidden": scatter_about(part_keys[0], (ATTEMPTS, MODEL_WIDTH), 1.0, 6.0, ((0, 4), (1, 4))),
        "base_query_projection": draw_base_query_projection(jax.random.fold_in(jax.random.fold_in(key_list[13], part), 71), part),
        "base_key_projection": scatter_about(part_keys[2], (ATTEMPTS, ATTENTION_HEADS * HEAD_SIZE), 1.0, 6.0, ((0, 4), (1, 4))),
        "base_value_projection": scatter_about(part_keys[3], (ATTEMPTS, ATTENTION_HEADS * HEAD_SIZE), 1.0, 6.0, ((0, 4), (1, 4))),
        "adapter_input_factors": scatter_about(part_keys[4], (THEOREM_VARIANTS, MODEL_WIDTH, 2 * ADAPTER_RANK), MODEL_WIDTH ** -0.5, 0.09375, ((0, 4), (1, 4))),
        "adapter_output_factors": scatter_about(part_keys[5], (THEOREM_VARIANTS, 2, ADAPTER_RANK, ATTENTION_HEADS * HEAD_SIZE), ADAPTER_RANK ** -0.5, 0.75, ((0, 4), (3, 4))),
        "statement_prefix_cache": scatter_about(part_keys[6], (BLOCKS, 2, BLK, ATTENTION_HEADS * HEAD_SIZE), 1.0, 6.0, ((0, 4), (3, 4))),
        "generated_token_cache": scatter_about(part_keys[7], (ATTEMPTS, 2, SUFFIX, ATTENTION_HEADS * HEAD_SIZE), 1.0, 6.0, ((0, 4), (3, 4))),
        "attempt_theorem_index": draw_attempt_theorem_index(jax.random.fold_in(jax.random.fold_in(key_list[13], part), 71), part),
        "host_live_count": draw_host_live_count(jax.random.fold_in(jax.random.fold_in(key_list[13], part), 71), part),
        "adapter_pool_row": draw_adapter_pool_row(jax.random.fold_in(jax.random.fold_in(key_list[13], part), 71), part),
        "prefix_pool_row": draw_prefix_pool_row(jax.random.fold_in(jax.random.fold_in(key_list[13], part), 71), part),
        "prefix_block_count": draw_prefix_block_count(jax.random.fold_in(jax.random.fold_in(key_list[13], part), 71), part),
    }


ADAPTER_SCALE = 0.5
ROPE_BASE = 10000.0
NEG_FILL = -1.0e30


def rotate(values, position):
    shaped = values.reshape(values.shape[:-1] + (-1, HEAD_SIZE))
    halfway = HEAD_SIZE // 2
    frequency = ROPE_BASE ** (-(jnp.arange(halfway, dtype=jnp.float32) * (2.0 / HEAD_SIZE)))
    angles = position.astype(jnp.float32)[..., None] * frequency
    cosine = jnp.cos(angles)[..., None, :]
    sine_part = jnp.sin(angles)[..., None, :]
    first_half = shaped[..., :halfway]
    second = shaped[..., halfway:]
    turned = jnp.concatenate([first_half * cosine - second * sine_part, second * cosine + first_half * sine_part], axis=-1)
    return turned.reshape(values.shape)


def reference(hidden, base_query_projection, base_key_projection, base_value_projection, adapter_input_factors, adapter_output_factors, statement_prefix_cache, generated_token_cache, attempt_theorem_index, host_live_count, adapter_pool_row, prefix_pool_row, prefix_block_count):
    adapter_rows = adapter_pool_row[attempt_theorem_index]
    block_rows = prefix_pool_row[attempt_theorem_index]
    block_counts = prefix_block_count[attempt_theorem_index]
    row_width = ATTENTION_HEADS * HEAD_SIZE

    def one_attempt(packet):
        hidden_state_row, query_row, key_row, value_row, suffix_rows, adapter_position, block_list, block_count = packet
        adapter_rank_row = jnp.dot(hidden_state_row, adapter_input_factors[adapter_position], preferred_element_type=jnp.float32).astype(jnp.bfloat16)
        output_factor = adapter_output_factors[adapter_position]
        query_correction = (jnp.dot(adapter_rank_row[:ADAPTER_RANK], output_factor[0], preferred_element_type=jnp.float32) * ADAPTER_SCALE).astype(jnp.bfloat16)
        value_correction = (jnp.dot(adapter_rank_row[ADAPTER_RANK:], output_factor[1], preferred_element_type=jnp.float32) * ADAPTER_SCALE).astype(jnp.bfloat16)
        position = BLK * block_count + SUFFIX
        query_vector = rotate(query_row.astype(jnp.float32) + query_correction.astype(jnp.float32), position).astype(jnp.bfloat16)
        new_key = rotate(key_row.astype(jnp.float32), position).astype(jnp.bfloat16)
        new_value = (value_row.astype(jnp.float32) + value_correction.astype(jnp.float32)).astype(jnp.bfloat16)
        heads_query = query_vector.reshape(ATTENTION_HEADS, HEAD_SIZE).astype(jnp.float32)
        chosen = statement_prefix_cache[block_list]
        block_keys = chosen[:, 0].reshape(PBLK, BLK, ATTENTION_HEADS, HEAD_SIZE).astype(jnp.float32)
        block_values = chosen[:, 1].reshape(PBLK, BLK, ATTENTION_HEADS, HEAD_SIZE).astype(jnp.float32)
        scores = jnp.einsum("hd,bthd->bht", heads_query, block_keys) * (HEAD_SIZE ** -0.5)
        usable = jnp.arange(PBLK, dtype=jnp.int32) < block_count
        peak_score = jnp.where(usable[:, None], jnp.max(scores, axis=2), NEG_FILL)
        weights = jnp.where(usable[:, None, None], jnp.exp(scores - peak_score[..., None]), 0.0)
        totals = jnp.sum(weights, axis=2)
        rounded = lax.optimization_barrier(weights.astype(jnp.bfloat16)).astype(jnp.float32)
        mixed_rows = jnp.einsum("bht,bthd->bhd", rounded, block_values)
        own_keys = jnp.concatenate([suffix_rows[0], new_key[None, :]], axis=0).reshape(SUFFIX + 1, ATTENTION_HEADS, HEAD_SIZE).astype(jnp.float32)
        own_values = jnp.concatenate([suffix_rows[1], new_value[None, :]], axis=0).reshape(SUFFIX + 1, ATTENTION_HEADS, HEAD_SIZE).astype(jnp.float32)
        own_scores = jnp.einsum("hd,thd->ht", heads_query, own_keys) * (HEAD_SIZE ** -0.5)
        own_peak = jnp.max(own_scores, axis=1)
        own_weights = jnp.exp(own_scores - own_peak[:, None])
        own_totals = jnp.sum(own_weights, axis=1)
        own_rounded = lax.optimization_barrier(own_weights.astype(jnp.bfloat16)).astype(jnp.float32)
        own_mixed = jnp.einsum("ht,thd->hd", own_rounded, own_values)
        overall = jnp.maximum(jnp.max(peak_score, axis=0), own_peak)
        prefix_factor = jnp.exp(peak_score - overall[None, :])
        own_factor = jnp.exp(own_peak - overall)
        numerator = jnp.sum(mixed_rows * prefix_factor[..., None], axis=0) + own_mixed * own_factor[:, None]
        denominator = jnp.sum(totals * prefix_factor, axis=0) + own_totals * own_factor
        result = (numerator / denominator[:, None]).reshape(row_width).astype(jnp.bfloat16)
        return result, new_key, new_value

    attended, key_rows, value_rows = lax.map(one_attempt, (hidden, base_query_projection, base_key_projection, base_value_projection, generated_token_cache, adapter_rows, block_rows, block_counts))
    ordinal = jnp.arange(ATTEMPTS, dtype=jnp.int32)
    living = (ordinal % ATT_DEV) < host_live_count[ordinal // ATT_DEV]
    live_rows = living[:, None]
    return (jnp.where(live_rows, attended, 0.0).astype(jnp.bfloat16), jnp.where(live_rows, key_rows, 0.0).astype(jnp.bfloat16), jnp.where(live_rows, value_rows, 0.0).astype(jnp.bfloat16))
```

```python
import jax
import jax.numpy as jnp
from jax import lax
from jax.experimental import pallas as pl
from jax.experimental.pallas import tpu as pltpu
from jax.sharding import PartitionSpec as P

HEAD_SIZE = 128
ADAPTER_RANK = 64
BLK = 128
PBLK = 4


ADAPTER_SCALE = 0.5
ROPE_BASE = 10000.0
NEG_FILL = -1e30


def rotate(values, position):
    shaped = values.reshape(values.shape[:-1] + (-1, HEAD_SIZE))
    halfway = HEAD_SIZE // 2
    frequency = ROPE_BASE ** (-(jnp.arange(halfway, dtype=jnp.float32) * (2.0 / HEAD_SIZE)))
    angles = position.astype(jnp.float32)[..., None] * frequency
    cosine = jnp.cos(angles)[..., None, :]
    sine_part = jnp.sin(angles)[..., None, :]
    first_half = shaped[..., :halfway]
    second = shaped[..., halfway:]
    turned = jnp.concatenate(
        [first_half * cosine - second * sine_part, second * cosine + first_half * sine_part],
        axis=-1,
    )
    return turned.reshape(values.shape)


def lookup_table(source_table, wanted):
    matches = wanted[:, None] == jnp.arange(source_table.shape[0], dtype=jnp.int32)[None, :]
    if source_table.ndim == 1:
        return jnp.sum(jnp.where(matches, source_table[None, :], 0), axis=1)
    return jnp.sum(jnp.where(matches[:, :, None], source_table[None, :, :], 0), axis=1)


def route_matrix(destination, validity, capacity, host_total):
    ordinal = jnp.arange(destination.shape[0], dtype=jnp.int32)
    earlier = (
        (destination[:, None] == destination[None, :])
        & validity[None, :]
        & (ordinal[None, :] < ordinal[:, None])
    )
    ranking = jnp.sum(earlier.astype(jnp.int32), axis=1)
    target = destination * capacity + ranking
    places = jnp.arange(host_total * capacity, dtype=jnp.int32)
    return ((places[:, None] == target[None, :]) & validity[None, :]).astype(jnp.bfloat16)


def pack_rows(router, payload):
    return jnp.dot(router, payload, preferred_element_type=jnp.float32).astype(jnp.bfloat16)


def attend_local(queries, chosen, statement_prefix_cache):
    head_count = queries.shape[-1] // HEAD_SIZE
    blocks = statement_prefix_cache.shape[0]
    block_keys = statement_prefix_cache[:, 0].reshape(
        blocks, statement_prefix_cache.shape[2], head_count, HEAD_SIZE
    )
    block_values = statement_prefix_cache[:, 1].reshape(
        blocks, statement_prefix_cache.shape[2], head_count, HEAD_SIZE
    )
    shaped = queries.reshape(queries.shape[:-1] + (head_count, HEAD_SIZE))
    scores = jnp.einsum(
        "nchd,bthd->ncbht", shaped, block_keys, preferred_element_type=jnp.float32
    ) * HEAD_SIZE ** (-0.5)
    chosen_mask = (chosen > 0)[:, :, :, None, None]
    masked = jnp.where(chosen_mask, scores, NEG_FILL)
    top_score = jnp.max(masked, axis=(2, 4))
    weights = jnp.where(chosen_mask, jnp.exp(masked - top_score[:, :, None, :, None]), 0.0)
    totals = jnp.sum(weights, axis=(2, 4))
    mixed_rows = jnp.einsum(
        "ncbht,bthd->nchd",
        weights.astype(jnp.bfloat16),
        block_values,
        preferred_element_type=jnp.float32,
    )
    return (mixed_rows.reshape(queries.shape), top_score, totals)


def routed_body(
    hidden,
    base_query_projection,
    base_key_projection,
    base_value_projection,
    adapter_input_factors,
    adapter_output_factors,
    statement_prefix_cache,
    generated_token_cache,
    attempt_theorem_index,
    host_live_count,
    adapter_pool_row,
    prefix_pool_row,
    prefix_block_count,
):
    host_total = lax.axis_size("hosts")
    attempts = hidden.shape[0]
    capacity = max(1, attempts // host_total)
    owner_held_rows = adapter_input_factors.shape[0]
    local_blocks = statement_prefix_cache.shape[0]
    row_width = base_query_projection.shape[1]
    head_count = row_width // HEAD_SIZE
    ordinal = jnp.arange(attempts, dtype=jnp.int32)
    living = ordinal < host_live_count[0]
    adapter_rows = lookup_table(adapter_pool_row, attempt_theorem_index)
    block_rows = lookup_table(prefix_pool_row, attempt_theorem_index)
    block_counts = lookup_table(prefix_block_count, attempt_theorem_index)
    position = BLK * block_counts + generated_token_cache.shape[2]
    adapter_router = route_matrix(adapter_rows // owner_held_rows, living, capacity, host_total)
    adapter_pick = (
        adapter_rows[:, None] % owner_held_rows
        == jnp.arange(owner_held_rows, dtype=jnp.int32)[None, :]
    ).astype(jnp.bfloat16)
    sent_hidden = pack_rows(adapter_router, hidden).reshape(host_total, capacity, hidden.shape[1])
    sent_pick = pack_rows(adapter_router, adapter_pick).reshape(
        host_total, capacity, owner_held_rows
    )
    incoming_rows = lax.all_to_all(sent_hidden, "hosts", split_axis=0, concat_axis=0, tiled=True)
    pick_in = lax.all_to_all(sent_pick, "hosts", split_axis=0, concat_axis=0, tiled=True)
    projected_rows = jnp.einsum(
        "xjp,epk->xjek", incoming_rows, adapter_input_factors, preferred_element_type=jnp.float32
    )
    partial_rank = jnp.sum(projected_rows * pick_in.astype(jnp.float32)[..., None], axis=2)
    rank_rows = lax.psum(partial_rank, "mp").astype(jnp.bfloat16)
    spread_rows = rank_rows[:, :, None, :] * pick_in[..., None]
    query_correction = jnp.einsum(
        "exqw,qwf->exf",
        spread_rows[..., :ADAPTER_RANK],
        adapter_output_factors[:, 0],
        preferred_element_type=jnp.float32,
    )
    value_correction = jnp.einsum(
        "exqw,qwf->exf",
        spread_rows[..., ADAPTER_RANK:],
        adapter_output_factors[:, 1],
        preferred_element_type=jnp.float32,
    )
    adapter_corrections = (
        jnp.concatenate([query_correction, value_correction], axis=-1) * ADAPTER_SCALE
    ).astype(jnp.bfloat16)
    returned = lax.all_to_all(adapter_corrections, "hosts", split_axis=0, concat_axis=0, tiled=True)
    adapter_corrections = jnp.dot(
        adapter_router.T,
        returned.reshape(host_total * capacity, 2 * row_width),
        preferred_element_type=jnp.float32,
    )
    query_rows = rotate(
        base_query_projection.astype(jnp.float32) + adapter_corrections[:, :row_width], position
    ).astype(jnp.bfloat16)
    value_rows = (
        base_value_projection.astype(jnp.float32) + adapter_corrections[:, row_width:]
    ).astype(jnp.bfloat16)
    key_rows = rotate(base_key_projection.astype(jnp.float32), position).astype(jnp.bfloat16)
    requests = []
    for block_index in range(PBLK):
        wanted = living & (block_index < block_counts)
        holder = block_rows[:, block_index]
        router = route_matrix(holder // local_blocks, wanted, capacity, host_total)
        block_pick = (
            holder[:, None] % local_blocks == jnp.arange(local_blocks, dtype=jnp.int32)[None, :]
        ).astype(jnp.bfloat16)
        sent_queries = pack_rows(router, query_rows).reshape(host_total, capacity, row_width)
        sent_blocks = pack_rows(router, block_pick).reshape(host_total, capacity, local_blocks)
        requests.append((router, wanted, sent_queries, sent_blocks))
    partials = []
    for request in requests:
        answer_mixed_rows, answer_top_score, answer_totals = attend_local(
            lax.all_to_all(request[2], "hosts", split_axis=0, concat_axis=0, tiled=True),
            lax.all_to_all(request[3], "hosts", split_axis=0, concat_axis=0, tiled=True),
            statement_prefix_cache,
        )
        partials.append(
            (
                lax.all_to_all(answer_mixed_rows, "hosts", split_axis=0, concat_axis=0, tiled=True),
                lax.all_to_all(answer_top_score, "hosts", split_axis=0, concat_axis=0, tiled=True),
                lax.all_to_all(answer_totals, "hosts", split_axis=0, concat_axis=0, tiled=True),
            )
        )
    entries = []
    for block_index in range(PBLK):
        router, wanted = (requests[block_index][0], requests[block_index][1])
        mixed_rows, top_score, totals = partials[block_index]
        back_router = router.T.astype(jnp.float32)
        flat_mixed = jnp.dot(
            back_router,
            mixed_rows.reshape(host_total * capacity, row_width),
            precision=lax.Precision.HIGHEST,
        )
        flat_top = jnp.dot(
            back_router,
            top_score.reshape(host_total * capacity, head_count),
            precision=lax.Precision.HIGHEST,
        )
        flat_totals = jnp.dot(
            back_router,
            totals.reshape(host_total * capacity, head_count),
            precision=lax.Precision.HIGHEST,
        )
        flat_top = jnp.where(wanted[:, None], flat_top, NEG_FILL)
        entries.append((flat_mixed, flat_top, flat_totals))
    shaped_query = query_rows.reshape(attempts, head_count, HEAD_SIZE)
    own_keys = jnp.concatenate([generated_token_cache[:, 0], key_rows[:, None, :]], axis=1).reshape(
        attempts, -1, head_count, HEAD_SIZE
    )
    own_values = jnp.concatenate(
        [generated_token_cache[:, 1], value_rows[:, None, :]], axis=1
    ).reshape(attempts, -1, head_count, HEAD_SIZE)
    own_scores = jnp.einsum(
        "ahd,athd->aht", shaped_query, own_keys, preferred_element_type=jnp.float32
    ) * HEAD_SIZE ** (-0.5)
    own_top = jnp.max(own_scores, axis=2)
    own_weights = jnp.exp(own_scores - own_top[..., None])
    own_totals = jnp.sum(own_weights, axis=2)
    own_mixed = jnp.einsum(
        "aht,athd->ahd",
        own_weights.astype(jnp.bfloat16),
        own_values,
        preferred_element_type=jnp.float32,
    )
    overall = own_top
    for flat_mixed, flat_top, flat_totals in entries:
        overall = jnp.maximum(overall, flat_top)
    own_factor = jnp.exp(own_top - overall)
    numerator = own_mixed * own_factor[..., None]
    denominator = own_totals * own_factor
    for flat_mixed, flat_top, flat_totals in entries:
        factor = jnp.exp(flat_top - overall)
        numerator = (
            numerator + flat_mixed.reshape(attempts, head_count, HEAD_SIZE) * factor[..., None]
        )
        denominator = denominator + flat_totals * factor
    attended = (numerator / denominator[..., None]).reshape(attempts, row_width)
    live_rows = living[:, None]
    return (
        jnp.where(live_rows, attended, 0.0).astype(jnp.bfloat16),
        jnp.where(live_rows, key_rows, 0.0),
        jnp.where(live_rows, value_rows, 0.0),
    )


SMEM = pl.BlockSpec(memory_space=pltpu.SMEM)
VMEM = pl.BlockSpec(memory_space=pltpu.VMEM)
F32 = jnp.float32
BF16 = jnp.bfloat16


def shape_of(*dims, kind=BF16):
    return jax.ShapeDtypeStruct(dims, kind)


def host_offset(value, total):
    return jnp.where(value < 0, value + total, value)


def place_attempts(me, total, capacity, theorem_ref, live_ref, owner_ref, taken_ref):
    for r in range(total):
        taken_ref[r] = 0
    live = live_ref[0]
    slots = []
    for a in range(theorem_ref.shape[0]):
        r = host_offset(owner_ref[theorem_ref[a]] - me, total)
        k = taken_ref[r]
        fits = jnp.logical_and(a < live, k < capacity)
        taken_ref[r] = jnp.where(fits, k + 1, k)
        slots.append(jnp.where(fits, r * capacity + k, -1))
    return slots


def pack_matrix(slots, slot_total):
    lanes = lax.broadcasted_iota(jnp.int32, (8, 128), 1)
    rows = lax.broadcasted_iota(jnp.int32, (8, 128), 0)
    wanted = jnp.full((8, 128), -1, jnp.int32)
    for a, slot in enumerate(slots):
        wanted = jnp.where(lanes == a, slot, wanted)
    pieces = [
        jnp.where(wanted == rows + base, 1.0, 0.0).astype(F32) for base in range(0, slot_total, 8)
    ]
    return jnp.concatenate(pieces, axis=0)[:, : len(slots)].astype(BF16)


def unpack_matrix(slots, slot_total):
    lanes = lax.broadcasted_iota(jnp.int32, (8, 128), 1)
    rows = lax.broadcasted_iota(jnp.int32, (8, 128), 0)
    pieces = []
    for base in range(0, len(slots), 8):
        wanted = jnp.full((8, 128), -1, jnp.int32)
        for k in range(8):
            wanted = jnp.where(rows == k, slots[base + k], wanted)
        pieces.append(jnp.where(wanted == lanes, 1.0, 0.0).astype(F32))
    return jnp.concatenate(pieces, axis=0)[:, :slot_total].astype(BF16)


def dot(left, right):
    return jnp.dot(left, right, preferred_element_type=F32)


def turn(values, cosine, sine):
    parts = []
    for base in range(0, values.shape[1], HEAD_SIZE):
        piece = values[:, base : base + HEAD_SIZE]
        parts.append(piece * cosine + pltpu.roll(piece, HEAD_SIZE // 2, 1) * sine)
    return jnp.concatenate(parts, axis=1)


def send_kernel(total, capacity, theorem_ref, live_ref, owner_ref, hidden_ref, query_ref, *rest):
    outs, taken_ref = rest[:total], rest[total]
    me = lax.axis_index("hosts")
    slots = place_attempts(me, total, capacity, theorem_ref, live_ref, owner_ref, taken_ref)
    router = pack_matrix(slots, total * capacity)
    packed_hidden = dot(router, hidden_ref[...])
    packed_query = dot(router, query_ref[...])
    for r in range(total):
        rows = slice(r * capacity, (r + 1) * capacity)
        outs[r][...] = jnp.concatenate([packed_hidden[rows], packed_query[rows]], axis=0).astype(
            BF16
        )


def table_kernel(
    total,
    capacity,
    theorem_ref,
    live_ref,
    owner_ref,
    prefix_ref,
    count_ref,
    key_ref,
    value_ref,
    cosine_ref,
    sine_ref,
    key_rows_ref,
    new_key_ref,
    packed_value_ref,
    unpack_ref,
    meta_ref,
    taken_ref,
):
    me = lax.axis_index("hosts")
    slot_total = total * capacity
    theorems = owner_ref.shape[0]
    blocks = theorems * PBLK // total
    slots = place_attempts(me, total, capacity, theorem_ref, live_ref, owner_ref, taken_ref)
    for s in range(slot_total):
        meta_ref[s] = 0
    for a, slot in enumerate(slots):
        meta_ref[jnp.where(slot < 0, meta_ref.shape[0] - 1, slot)] = a
    source_base, valid_base, place_base = slot_total, slot_total + blocks, slot_total + 2 * blocks
    spare = meta_ref.shape[0] - 1
    for t in range(theorems):
        owner = owner_ref[t]
        r = host_offset(owner - me, total)
        for j in range(PBLK):
            block = prefix_ref[t, j]
            holder = block // blocks
            inner = block - holder * blocks
            mine = holder == me
            meta_ref[jnp.where(mine, source_base + inner, spare)] = host_offset(me - owner, total)
            meta_ref[jnp.where(mine, valid_base + inner, spare)] = jnp.where(j < count_ref[t], 1, 0)
            meta_ref[place_base + r * PBLK + j] = host_offset(me - holder, total) * blocks + inner
    router = pack_matrix(slots, slot_total)
    back = unpack_matrix(slots, slot_total)
    unpack_ref[...] = back
    packed_value_ref[...] = dot(router, value_ref[...]).astype(BF16)
    packed_key = dot(router, key_ref[...])
    turned = []
    for r in range(total):
        turned.append(
            turn(
                packed_key[r * capacity : (r + 1) * capacity],
                cosine_ref[r : r + 1, :],
                sine_ref[r : r + 1, :],
            )
        )
    new_key = jnp.concatenate(turned, axis=0).astype(BF16)
    new_key_ref[...] = new_key
    key_rows_ref[...] = dot(back, new_key).astype(BF16)


def rank_kernel(total, capacity, *refs):
    rows, factors_ref, out_ref = refs[:total], refs[total], refs[total + 1]
    stacked = jnp.concatenate([ref[...] for ref in rows], axis=0)
    product = dot(stacked, factors_ref[...])
    out_ref[...] = jnp.concatenate(
        [product[2 * capacity * s : 2 * capacity * s + capacity] for s in range(total)], axis=0
    )


def query_kernel(total, capacity, sums, *refs):
    rows = refs[:total]
    partials = refs[total : total + sums]
    factors_ref, cosine_ref, sine_ref = refs[total + sums : total + sums + 3]
    outs = refs[total + sums + 3 :]
    slot_total = total * capacity
    level = [ref[...] for ref in partials]
    while len(level) > 1:
        level = [level[i] + level[i + 1] for i in range(0, len(level), 2)]
    rank = level[0].astype(BF16).astype(F32)
    lanes = lax.broadcasted_iota(jnp.int32, rank.shape, 1)
    split = jnp.concatenate(
        [jnp.where(lanes < ADAPTER_RANK, rank, 0.0), jnp.where(lanes < ADAPTER_RANK, 0.0, rank)],
        axis=0,
    ).astype(BF16)
    correction = (dot(split, factors_ref[...]) * ADAPTER_SCALE).astype(BF16).astype(F32)
    base = jnp.concatenate([ref[...].astype(F32)[capacity:] for ref in rows], axis=0)
    query = turn(base + correction[:slot_total], cosine_ref[0:1, :], sine_ref[0:1, :])
    for s in range(total):
        back = (total - s) % total
        first = slot_total + back * capacity
        outs[s][...] = jnp.concatenate(
            [query, correction[first : first + capacity]], axis=0
        ).astype(BF16)


def prefix_kernel(total, capacity, meta_ref, cache_ref, *refs):
    received, outs = refs[:total], refs[total : 2 * total]
    queries_ref, mixed_ref = refs[2 * total :]
    slot_total = total * capacity
    blocks, _, tokens, width = cache_ref.shape
    heads = width // HEAD_SIZE
    for s in range(total):
        queries_ref[s * slot_total : (s + 1) * slot_total, :] = received[s][0:slot_total, :]
    lanes = lax.broadcasted_iota(jnp.int32, (slot_total, HEAD_SIZE), 1)
    for b in range(blocks):
        source = meta_ref[slot_total + b]
        valid = meta_ref[slot_total + blocks + b]
        query = queries_ref[pl.ds(pl.multiple_of(source * slot_total, slot_total), slot_total), :]
        stats = jnp.zeros((slot_total, HEAD_SIZE), F32)
        for h in range(heads):
            part = slice(h * HEAD_SIZE, (h + 1) * HEAD_SIZE)
            scores = lax.dot_general(
                query[:, part],
                cache_ref[b, 0, :, part],
                (((1,), (1,)), ((), ())),
                preferred_element_type=F32,
            ) * HEAD_SIZE ** (-0.5)
            peak = jnp.max(scores, axis=1, keepdims=True)
            weights = jnp.exp(scores - peak)
            sums = jnp.sum(weights, axis=1, keepdims=True)
            stats = jnp.where(lanes == h, peak, stats)
            stats = jnp.where(lanes == heads + h, sums, stats)
            mixed_ref[b, :, part] = dot(weights.astype(BF16), cache_ref[b, 1, :, part])
        stats = jnp.where(jnp.logical_and(valid == 0, lanes < heads), NEG_FILL, stats)
        high = stats.astype(BF16).astype(F32)
        rest = stats - high
        middle = rest.astype(BF16).astype(F32)
        low = rest - middle
        mixed_ref[b, :, width:] = (
            high + pltpu.roll(middle, 2 * heads, 1) + pltpu.roll(low, 4 * heads, 1)
        )
        for s in range(total):
            group = host_offset(host_offset(-source, total) - s, total)
            outs[s][b] = mixed_ref[
                b, pl.ds(pl.multiple_of(group * capacity, capacity), capacity), :
            ].astype(BF16)


def head_ones(width, transposed):
    heads = width // HEAD_SIZE
    if transposed:
        rows = lax.broadcasted_iota(jnp.int32, (HEAD_SIZE, width), 0)
        features = lax.broadcasted_iota(jnp.int32, (HEAD_SIZE, width), 1)
    else:
        rows = lax.broadcasted_iota(jnp.int32, (width, HEAD_SIZE), 1)
        features = lax.broadcasted_iota(jnp.int32, (width, HEAD_SIZE), 0)
    inside = jnp.logical_and(features >= rows * HEAD_SIZE, features < (rows + 1) * HEAD_SIZE)
    return jnp.where(inside, 1.0, 0.0).astype(BF16)


def head_sums(products, ones):
    high = products.astype(BF16)
    low = (products - high.astype(F32)).astype(BF16)
    return dot(high, ones) + dot(low, ones)


def own_kernel(total, capacity, meta_ref, cache_ref, new_key_ref, packed_value_ref, unpack_ref, *refs):
    received = refs[:total]
    value_rows_ref, mixed_ref, peak_ref, sums_ref, product_ref = refs[total:]
    slot_total = total * capacity
    suffix = cache_ref.shape[2]
    width = cache_ref.shape[3]
    ones = head_ones(width, False)
    spread = head_ones(width, True)
    queries, corrections = [], []
    for r in range(total):
        full = received[(total - r) % total][...].astype(F32)
        queries.append(full[r * capacity : (r + 1) * capacity])
        corrections.append(full[slot_total : slot_total + capacity])
    query = jnp.concatenate(queries, axis=0)
    new_value = (packed_value_ref[...].astype(F32) + jnp.concatenate(corrections, axis=0)).astype(
        BF16
    )
    value_rows_ref[...] = dot(unpack_ref[...], new_value).astype(BF16)
    for s in range(slot_total):
        keys = cache_ref[meta_ref[s], 0].astype(F32)
        product_ref[s * suffix : (s + 1) * suffix, :] = keys * query[s : s + 1, :]
    scale = HEAD_SIZE ** (-0.5)
    scores = (head_sums(product_ref[...], ones) * scale).reshape(slot_total, suffix, HEAD_SIZE)
    new_scores = head_sums(new_key_ref[...].astype(F32) * query, ones) * scale
    peak = jnp.maximum(jnp.max(scores, axis=1), new_scores)
    weights = jnp.exp(scores - peak[:, None, :])
    new_weights = jnp.exp(new_scores - peak)
    peak_ref[...] = peak
    sums_ref[...] = jnp.sum(weights, axis=1) + new_weights
    product_ref[...] = dot(weights.reshape(slot_total * suffix, HEAD_SIZE).astype(BF16), spread)
    mixed_ref[...] = dot(new_weights.astype(BF16), spread) * new_value.astype(F32)
    for s in range(slot_total):
        values = cache_ref[meta_ref[s], 1].astype(F32)
        mixed_ref[s : s + 1, :] += jnp.sum(
            product_ref[s * suffix : (s + 1) * suffix, :] * values, axis=0, keepdims=True
        )


def combine_kernel(total, capacity, meta_ref, unpack_ref, mixed_ref, peak_ref, sums_ref, *refs):
    received, out_ref, parts_ref = refs[:total], refs[total], refs[total + 1]
    slot_total = total * capacity
    blocks = received[0].shape[0]
    width = mixed_ref.shape[1]
    heads = width // HEAD_SIZE
    for s in range(total):
        parts_ref[s * blocks : (s + 1) * blocks] = received[s][...]
    results = []
    for r in range(total):
        rows = slice(r * capacity, (r + 1) * capacity)
        overall = peak_ref[rows, :]
        pieces = []
        for j in range(PBLK):
            place = meta_ref[slot_total + 2 * blocks + r * PBLK + j]
            coded = parts_ref[place, :, width:].astype(F32)
            stats = (
                coded
                + pltpu.roll(coded, HEAD_SIZE - 2 * heads, 1)
                + pltpu.roll(coded, HEAD_SIZE - 4 * heads, 1)
            )
            pieces.append((place, stats, pltpu.roll(stats, HEAD_SIZE - heads, 1)))
            overall = jnp.maximum(overall, stats)
        own_factor = jnp.exp(peak_ref[rows, :] - overall)
        denominator = sums_ref[rows, :] * own_factor
        factors = []
        for place, top, sums in pieces:
            factor = jnp.exp(top - overall)
            factors.append(factor)
            denominator = denominator + sums * factor
        columns = []
        for h in range(heads):
            part = slice(h * HEAD_SIZE, (h + 1) * HEAD_SIZE)
            numerator = mixed_ref[rows, part] * own_factor[:, h : h + 1]
            for (place, _, _), factor in zip(pieces, factors):
                numerator = numerator + parts_ref[place, :, part].astype(F32) * factor[:, h : h + 1]
            columns.append(numerator / denominator[:, h : h + 1])
        results.append(jnp.concatenate(columns, axis=1))
    attended = jnp.concatenate(results, axis=0).astype(BF16)
    out_ref[...] = dot(unpack_ref[...], attended).astype(BF16)


def exchange(arrays):
    total = len(arrays)
    received = [arrays[0]]
    for s in range(1, total):
        ring = [(i, (i + s) % total) for i in range(total)]
        received.append(lax.ppermute(arrays[s], "hosts", ring))
    return received


def direct_body(
    hidden,
    base_query_projection,
    base_key_projection,
    base_value_projection,
    adapter_input_factors,
    adapter_output_factors,
    statement_prefix_cache,
    generated_token_cache,
    attempt_theorem_index,
    host_live_count,
    adapter_pool_row,
    prefix_pool_row,
    prefix_block_count,
):
    total = lax.axis_size("hosts")
    shares = lax.axis_size("mp")
    attempts, width = hidden.shape
    capacity = attempts // total
    slot_total = total * capacity
    blocks = statement_prefix_cache.shape[0]
    suffix = generated_token_cache.shape[2]
    input_factors = adapter_input_factors[0]
    output_factors = adapter_output_factors.reshape(2 * ADAPTER_RANK, width)
    taken = pltpu.SMEM((total,), jnp.int32)

    sent = pl.pallas_call(
        lambda *refs: send_kernel(total, capacity, *refs),
        out_shape=[shape_of(2 * capacity, width)] * total,
        in_specs=[SMEM] * 3 + [VMEM] * 2,
        out_specs=[VMEM] * total,
        scratch_shapes=[taken],
        name="send_rows",
    )(attempt_theorem_index, host_live_count, adapter_pool_row, hidden, base_query_projection)
    rows = exchange(sent)

    me = lax.axis_index("hosts")
    owners = (me + jnp.arange(total, dtype=jnp.int32)) % total
    counts = jnp.sum(
        jnp.where(
            owners[:, None] == adapter_pool_row[None, :], prefix_block_count[None, :], 0
        ),
        axis=1,
    )
    position = (BLK * counts + suffix).astype(F32)
    frequency = ROPE_BASE ** (
        -(jnp.arange(HEAD_SIZE // 2, dtype=F32) * (2.0 / HEAD_SIZE))
    )
    angles = position[:, None] * frequency
    cosine = jnp.cos(angles)
    sine = jnp.sin(angles)
    cosine = jnp.concatenate([cosine, cosine], axis=1)
    sine = jnp.concatenate([-sine, sine], axis=1)

    key_rows, new_key, packed_value, unpack, meta = pl.pallas_call(
        lambda *refs: table_kernel(total, capacity, *refs),
        out_shape=[
            shape_of(attempts, width),
            shape_of(slot_total, width),
            shape_of(slot_total, width),
            shape_of(attempts, slot_total),
            shape_of(slot_total + 2 * blocks + total * PBLK + 1, kind=jnp.int32),
        ],
        in_specs=[SMEM] * 5 + [VMEM] * 4,
        out_specs=[VMEM] * 4 + [SMEM],
        scratch_shapes=[taken],
        name="slot_tables",
    )(
        attempt_theorem_index,
        host_live_count,
        adapter_pool_row,
        prefix_pool_row,
        prefix_block_count,
        base_key_projection,
        base_value_projection,
        cosine,
        sine,
    )

    partial = pl.pallas_call(
        lambda *refs: rank_kernel(total, capacity, *refs),
        out_shape=shape_of(slot_total, 2 * ADAPTER_RANK, kind=F32),
        in_specs=[VMEM] * (total + 1),
        out_specs=VMEM,
        name="rank_rows",
    )(*rows, input_factors)
    partials = [partial]
    for s in range(1, shares):
        partials.append(lax.ppermute(partial, "mp", [(i, i ^ s) for i in range(shares)]))

    answers = pl.pallas_call(
        lambda *refs: query_kernel(total, capacity, shares, *refs),
        out_shape=[shape_of(slot_total + capacity, width)] * total,
        in_specs=[VMEM] * (total + shares + 3),
        out_specs=[VMEM] * total,
        name="query_rows",
    )(*rows, *partials, output_factors, cosine, sine)
    queries = exchange(answers)

    replies = pl.pallas_call(
        lambda *refs: prefix_kernel(total, capacity, *refs),
        out_shape=[shape_of(blocks, capacity, width + HEAD_SIZE)] * total,
        in_specs=[SMEM] + [VMEM] * (total + 1),
        out_specs=[VMEM] * total,
        scratch_shapes=[
            pltpu.VMEM((total * slot_total, width), BF16),
            pltpu.VMEM((blocks, slot_total, width + HEAD_SIZE), F32),
        ],
        name="prefix_attention",
    )(meta, statement_prefix_cache, *queries)
    partial_rows = exchange(replies)

    value_rows, mixed, peak, sums = pl.pallas_call(
        lambda *refs: own_kernel(total, capacity, *refs),
        out_shape=[
            shape_of(attempts, width),
            shape_of(slot_total, width, kind=F32),
            shape_of(slot_total, HEAD_SIZE, kind=F32),
            shape_of(slot_total, HEAD_SIZE, kind=F32),
        ],
        in_specs=[SMEM] + [VMEM] * (total + 4),
        out_specs=[VMEM] * 4,
        scratch_shapes=[pltpu.VMEM((slot_total * suffix, width), F32)],
        name="own_attention",
    )(meta, generated_token_cache, new_key, packed_value, unpack, *queries)

    attended = pl.pallas_call(
        lambda *refs: combine_kernel(total, capacity, *refs),
        out_shape=shape_of(attempts, width),
        in_specs=[SMEM] + [VMEM] * (total + 4),
        out_specs=VMEM,
        scratch_shapes=[pltpu.VMEM((total * blocks, capacity, width + HEAD_SIZE), BF16)],
        name="combine",
    )(meta, unpack, mixed, peak, sums, *partial_rows)
    return attended, key_rows, value_rows


def body(*arguments):
    total = lax.axis_size("hosts")
    shares = lax.axis_size("mp")
    attempts, width = arguments[0].shape
    theorems = arguments[10].shape[0]
    blocks = arguments[6].shape[0]
    suffix = arguments[7].shape[2]
    direct = (
        total <= 8
        and shares & (shares - 1) == 0
        and arguments[4].shape[0] == 1
        and theorems == total
        and blocks * total == theorems * PBLK
        and attempts == 8 * total
        and 2 * total * 8 <= 128
        and suffix == 8
        and 6 * (width // HEAD_SIZE) <= HEAD_SIZE
    )
    return direct_body(*arguments) if direct else routed_body(*arguments)


def solution(mesh):
    placed = (
        P(("groups", "hosts"), "mp"),
        P(("groups", "hosts"), "mp"),
        P(("groups", "hosts"), "mp"),
        P(("groups", "hosts"), "mp"),
        P(("groups", "hosts"), "mp", None),
        P(("groups", "hosts"), None, None, "mp"),
        P(("groups", "hosts"), None, None, "mp"),
        P(("groups", "hosts"), None, None, "mp"),
        P(("groups", "hosts")),
        P(("groups", "hosts")),
        P("groups"),
        P("groups", None),
        P("groups"),
    )
    return jax.shard_map(
        body,
        mesh=mesh,
        in_specs=placed,
        out_specs=(
            P(("groups", "hosts"), "mp"),
            P(("groups", "hosts"), "mp"),
            P(("groups", "hosts"), "mp"),
        ),
        check_vma=False,
    )
```

```python
import jax
import jax.numpy as jnp
from jax import lax
from jax.experimental import pallas as pl
from jax.experimental.pallas import tpu as pltpu
from jax.sharding import PartitionSpec as P

HEAD_SIZE = 128
ADAPTER_RANK = 64
BLK = 128
PBLK = 4


ADAPTER_SCALE = 0.5
ROPE_BASE = 10000.0
NEG_FILL = -1e30


def rotate(values, position):
    shaped = values.reshape(values.shape[:-1] + (-1, HEAD_SIZE))
    halfway = HEAD_SIZE // 2
    frequency = ROPE_BASE ** (-(jnp.arange(halfway, dtype=jnp.float32) * (2.0 / HEAD_SIZE)))
    angles = position.astype(jnp.float32)[..., None] * frequency
    cosine = jnp.cos(angles)[..., None, :]
    sine_part = jnp.sin(angles)[..., None, :]
    first_half = shaped[..., :halfway]
    second = shaped[..., halfway:]
    turned = jnp.concatenate(
        [first_half * cosine - second * sine_part, second * cosine + first_half * sine_part],
        axis=-1,
    )
    return turned.reshape(values.shape)


def lookup_table(source_table, wanted):
    matches = wanted[:, None] == jnp.arange(source_table.shape[0], dtype=jnp.int32)[None, :]
    if source_table.ndim == 1:
        return jnp.sum(jnp.where(matches, source_table[None, :], 0), axis=1)
    return jnp.sum(jnp.where(matches[:, :, None], source_table[None, :, :], 0), axis=1)


def route_matrix(destination, validity, capacity, host_total):
    ordinal = jnp.arange(destination.shape[0], dtype=jnp.int32)
    earlier = (
        (destination[:, None] == destination[None, :])
        & validity[None, :]
        & (ordinal[None, :] < ordinal[:, None])
    )
    ranking = jnp.sum(earlier.astype(jnp.int32), axis=1)
    target = destination * capacity + ranking
    places = jnp.arange(host_total * capacity, dtype=jnp.int32)
    return ((places[:, None] == target[None, :]) & validity[None, :]).astype(jnp.bfloat16)


def pack_rows(router, payload):
    return jnp.dot(router, payload, preferred_element_type=jnp.float32).astype(jnp.bfloat16)


def attend_local(queries, chosen, statement_prefix_cache):
    head_count = queries.shape[-1] // HEAD_SIZE
    blocks = statement_prefix_cache.shape[0]
    block_keys = statement_prefix_cache[:, 0].reshape(
        blocks, statement_prefix_cache.shape[2], head_count, HEAD_SIZE
    )
    block_values = statement_prefix_cache[:, 1].reshape(
        blocks, statement_prefix_cache.shape[2], head_count, HEAD_SIZE
    )
    shaped = queries.reshape(queries.shape[:-1] + (head_count, HEAD_SIZE))
    scores = jnp.einsum(
        "nchd,bthd->ncbht", shaped, block_keys, preferred_element_type=jnp.float32
    ) * HEAD_SIZE ** (-0.5)
    chosen_mask = (chosen > 0)[:, :, :, None, None]
    masked = jnp.where(chosen_mask, scores, NEG_FILL)
    top_score = jnp.max(masked, axis=(2, 4))
    weights = jnp.where(chosen_mask, jnp.exp(masked - top_score[:, :, None, :, None]), 0.0)
    totals = jnp.sum(weights, axis=(2, 4))
    mixed_rows = jnp.einsum(
        "ncbht,bthd->nchd",
        weights.astype(jnp.bfloat16),
        block_values,
        preferred_element_type=jnp.float32,
    )
    return (mixed_rows.reshape(queries.shape), top_score, totals)


def routed_body(
    hidden,
    base_query_projection,
    base_key_projection,
    base_value_projection,
    adapter_input_factors,
    adapter_output_factors,
    statement_prefix_cache,
    generated_token_cache,
    attempt_theorem_index,
    host_live_count,
    adapter_pool_row,
    prefix_pool_row,
    prefix_block_count,
):
    host_total = lax.axis_size("hosts")
    attempts = hidden.shape[0]
    capacity = max(1, attempts // host_total)
    owner_held_rows = adapter_input_factors.shape[0]
    local_blocks = statement_prefix_cache.shape[0]
    row_width = base_query_projection.shape[1]
    head_count = row_width // HEAD_SIZE
    ordinal = jnp.arange(attempts, dtype=jnp.int32)
    living = ordinal < host_live_count[0]
    adapter_rows = lookup_table(adapter_pool_row, attempt_theorem_index)
    block_rows = lookup_table(prefix_pool_row, attempt_theorem_index)
    block_counts = lookup_table(prefix_block_count, attempt_theorem_index)
    position = BLK * block_counts + generated_token_cache.shape[2]
    adapter_router = route_matrix(adapter_rows // owner_held_rows, living, capacity, host_total)
    adapter_pick = (
        adapter_rows[:, None] % owner_held_rows
        == jnp.arange(owner_held_rows, dtype=jnp.int32)[None, :]
    ).astype(jnp.bfloat16)
    sent_hidden = pack_rows(adapter_router, hidden).reshape(host_total, capacity, hidden.shape[1])
    sent_pick = pack_rows(adapter_router, adapter_pick).reshape(
        host_total, capacity, owner_held_rows
    )
    incoming_rows = lax.all_to_all(sent_hidden, "hosts", split_axis=0, concat_axis=0, tiled=True)
    pick_in = lax.all_to_all(sent_pick, "hosts", split_axis=0, concat_axis=0, tiled=True)
    projected_rows = jnp.einsum(
        "xjp,epk->xjek", incoming_rows, adapter_input_factors, preferred_element_type=jnp.float32
    )
    partial_rank = jnp.sum(projected_rows * pick_in.astype(jnp.float32)[..., None], axis=2)
    rank_rows = lax.psum(partial_rank, "mp").astype(jnp.bfloat16)
    spread_rows = rank_rows[:, :, None, :] * pick_in[..., None]
    query_correction = jnp.einsum(
        "exqw,qwf->exf",
        spread_rows[..., :ADAPTER_RANK],
        adapter_output_factors[:, 0],
        preferred_element_type=jnp.float32,
    )
    value_correction = jnp.einsum(
        "exqw,qwf->exf",
        spread_rows[..., ADAPTER_RANK:],
        adapter_output_factors[:, 1],
        preferred_element_type=jnp.float32,
    )
    adapter_corrections = (
        jnp.concatenate([query_correction, value_correction], axis=-1) * ADAPTER_SCALE
    ).astype(jnp.bfloat16)
    returned = lax.all_to_all(adapter_corrections, "hosts", split_axis=0, concat_axis=0, tiled=True)
    adapter_corrections = jnp.dot(
        adapter_router.T,
        returned.reshape(host_total * capacity, 2 * row_width),
        preferred_element_type=jnp.float32,
    )
    query_rows = rotate(
        base_query_projection.astype(jnp.float32) + adapter_corrections[:, :row_width], position
    ).astype(jnp.bfloat16)
    value_rows = (
        base_value_projection.astype(jnp.float32) + adapter_corrections[:, row_width:]
    ).astype(jnp.bfloat16)
    key_rows = rotate(base_key_projection.astype(jnp.float32), position).astype(jnp.bfloat16)
    requests = []
    for block_index in range(PBLK):
        wanted = living & (block_index < block_counts)
        holder = block_rows[:, block_index]
        router = route_matrix(holder // local_blocks, wanted, capacity, host_total)
        block_pick = (
            holder[:, None] % local_blocks == jnp.arange(local_blocks, dtype=jnp.int32)[None, :]
        ).astype(jnp.bfloat16)
        sent_queries = pack_rows(router, query_rows).reshape(host_total, capacity, row_width)
        sent_blocks = pack_rows(router, block_pick).reshape(host_total, capacity, local_blocks)
        requests.append((router, wanted, sent_queries, sent_blocks))
    partials = []
    for request in requests:
        answer_mixed_rows, answer_top_score, answer_totals = attend_local(
            lax.all_to_all(request[2], "hosts", split_axis=0, concat_axis=0, tiled=True),
            lax.all_to_all(request[3], "hosts", split_axis=0, concat_axis=0, tiled=True),
            statement_prefix_cache,
        )
        partials.append(
            (
                lax.all_to_all(answer_mixed_rows, "hosts", split_axis=0, concat_axis=0, tiled=True),
                lax.all_to_all(answer_top_score, "hosts", split_axis=0, concat_axis=0, tiled=True),
                lax.all_to_all(answer_totals, "hosts", split_axis=0, concat_axis=0, tiled=True),
            )
        )
    entries = []
    for block_index in range(PBLK):
        router, wanted = (requests[block_index][0], requests[block_index][1])
        mixed_rows, top_score, totals = partials[block_index]
        back_router = router.T.astype(jnp.float32)
        flat_mixed = jnp.dot(
            back_router,
            mixed_rows.reshape(host_total * capacity, row_width),
            precision=lax.Precision.HIGHEST,
        )
        flat_top = jnp.dot(
            back_router,
            top_score.reshape(host_total * capacity, head_count),
            precision=lax.Precision.HIGHEST,
        )
        flat_totals = jnp.dot(
            back_router,
            totals.reshape(host_total * capacity, head_count),
            precision=lax.Precision.HIGHEST,
        )
        flat_top = jnp.where(wanted[:, None], flat_top, NEG_FILL)
        entries.append((flat_mixed, flat_top, flat_totals))
    shaped_query = query_rows.reshape(attempts, head_count, HEAD_SIZE)
    own_keys = jnp.concatenate([generated_token_cache[:, 0], key_rows[:, None, :]], axis=1).reshape(
        attempts, -1, head_count, HEAD_SIZE
    )
    own_values = jnp.concatenate(
        [generated_token_cache[:, 1], value_rows[:, None, :]], axis=1
    ).reshape(attempts, -1, head_count, HEAD_SIZE)
    own_scores = jnp.einsum(
        "ahd,athd->aht", shaped_query, own_keys, preferred_element_type=jnp.float32
    ) * HEAD_SIZE ** (-0.5)
    own_top = jnp.max(own_scores, axis=2)
    own_weights = jnp.exp(own_scores - own_top[..., None])
    own_totals = jnp.sum(own_weights, axis=2)
    own_mixed = jnp.einsum(
        "aht,athd->ahd",
        own_weights.astype(jnp.bfloat16),
        own_values,
        preferred_element_type=jnp.float32,
    )
    overall = own_top
    for flat_mixed, flat_top, flat_totals in entries:
        overall = jnp.maximum(overall, flat_top)
    own_factor = jnp.exp(own_top - overall)
    numerator = own_mixed * own_factor[..., None]
    denominator = own_totals * own_factor
    for flat_mixed, flat_top, flat_totals in entries:
        factor = jnp.exp(flat_top - overall)
        numerator = (
            numerator + flat_mixed.reshape(attempts, head_count, HEAD_SIZE) * factor[..., None]
        )
        denominator = denominator + flat_totals * factor
    attended = (numerator / denominator[..., None]).reshape(attempts, row_width)
    live_rows = living[:, None]
    return (
        jnp.where(live_rows, attended, 0.0).astype(jnp.bfloat16),
        jnp.where(live_rows, key_rows, 0.0),
        jnp.where(live_rows, value_rows, 0.0),
    )


SMEM = pl.BlockSpec(memory_space=pltpu.SMEM)
VMEM = pl.BlockSpec(memory_space=pltpu.VMEM)
GRANT = pltpu.CompilerParams(vmem_limit_bytes=16 * 1024 * 1024)
F32 = jnp.float32
BF16 = jnp.bfloat16


def shape_of(*dims, kind=BF16):
    return jax.ShapeDtypeStruct(dims, kind)


def host_offset(value, total):
    return jnp.where(value < 0, value + total, value)


def place_attempts(me, total, capacity, theorem_ref, live_ref, owner_ref, taken_ref):
    for r in range(total):
        taken_ref[r] = 0
    live = live_ref[0]
    slots = []
    for a in range(theorem_ref.shape[0]):
        r = host_offset(owner_ref[theorem_ref[a]] - me, total)
        k = taken_ref[r]
        fits = jnp.logical_and(a < live, k < capacity)
        taken_ref[r] = jnp.where(fits, k + 1, k)
        slots.append(jnp.where(fits, r * capacity + k, -1))
    return slots


def pack_matrix(slots, slot_total):
    lanes = lax.broadcasted_iota(jnp.int32, (8, 128), 1)
    rows = lax.broadcasted_iota(jnp.int32, (8, 128), 0)
    wanted = jnp.full((8, 128), -1, jnp.int32)
    for a, slot in enumerate(slots):
        wanted = jnp.where(lanes == a, slot, wanted)
    pieces = [
        jnp.where(wanted == rows + base, 1.0, 0.0).astype(F32) for base in range(0, slot_total, 8)
    ]
    return jnp.concatenate(pieces, axis=0)[:, : len(slots)].astype(BF16)


def unpack_matrix(slots, slot_total):
    lanes = lax.broadcasted_iota(jnp.int32, (8, 128), 1)
    rows = lax.broadcasted_iota(jnp.int32, (8, 128), 0)
    pieces = []
    for base in range(0, len(slots), 8):
        wanted = jnp.full((8, 128), -1, jnp.int32)
        for k in range(8):
            wanted = jnp.where(rows == k, slots[base + k], wanted)
        pieces.append(jnp.where(wanted == lanes, 1.0, 0.0).astype(F32))
    return jnp.concatenate(pieces, axis=0)[:, :slot_total].astype(BF16)


def dot(left, right):
    return jnp.dot(left, right, preferred_element_type=F32)


def turn(values, cosine, sine):
    parts = []
    for base in range(0, values.shape[1], HEAD_SIZE):
        piece = values[:, base : base + HEAD_SIZE]
        parts.append(piece * cosine + pltpu.roll(piece, HEAD_SIZE // 2, 1) * sine)
    return jnp.concatenate(parts, axis=1)


def send_kernel(total, capacity, theorem_ref, live_ref, owner_ref, hidden_ref, query_ref, *rest):
    outs, taken_ref = rest[:total], rest[total]
    me = lax.axis_index("hosts")
    slots = place_attempts(me, total, capacity, theorem_ref, live_ref, owner_ref, taken_ref)
    router = pack_matrix(slots, total * capacity)
    packed_hidden = dot(router, hidden_ref[...])
    packed_query = dot(router, query_ref[...])
    for r in range(total):
        rows = slice(r * capacity, (r + 1) * capacity)
        outs[r][...] = jnp.concatenate([packed_hidden[rows], packed_query[rows]], axis=0).astype(
            BF16
        )


def table_kernel(
    total,
    capacity,
    theorem_ref,
    live_ref,
    owner_ref,
    prefix_ref,
    count_ref,
    key_ref,
    value_ref,
    cosine_ref,
    sine_ref,
    key_rows_ref,
    new_key_ref,
    packed_value_ref,
    unpack_ref,
    meta_ref,
    taken_ref,
):
    me = lax.axis_index("hosts")
    slot_total = total * capacity
    theorems = owner_ref.shape[0]
    blocks = theorems * PBLK // total
    slots = place_attempts(me, total, capacity, theorem_ref, live_ref, owner_ref, taken_ref)
    for s in range(slot_total):
        meta_ref[s] = 0
    for a, slot in enumerate(slots):
        meta_ref[jnp.where(slot < 0, meta_ref.shape[0] - 1, slot)] = a
    source_base, valid_base, place_base = slot_total, slot_total + blocks, slot_total + 2 * blocks
    spare = meta_ref.shape[0] - 1
    for t in range(theorems):
        owner = owner_ref[t]
        r = host_offset(owner - me, total)
        for j in range(PBLK):
            block = prefix_ref[t, j]
            holder = block // blocks
            inner = block - holder * blocks
            mine = holder == me
            meta_ref[jnp.where(mine, source_base + inner, spare)] = host_offset(me - owner, total)
            meta_ref[jnp.where(mine, valid_base + inner, spare)] = jnp.where(j < count_ref[t], 1, 0)
            meta_ref[place_base + r * PBLK + j] = host_offset(me - holder, total) * blocks + inner
    router = pack_matrix(slots, slot_total)
    back = unpack_matrix(slots, slot_total)
    unpack_ref[...] = back
    packed_value_ref[...] = dot(router, value_ref[...]).astype(BF16)
    packed_key = dot(router, key_ref[...])
    turned = []
    for r in range(total):
        turned.append(
            turn(
                packed_key[r * capacity : (r + 1) * capacity],
                cosine_ref[r : r + 1, :],
                sine_ref[r : r + 1, :],
            )
        )
    new_key = jnp.concatenate(turned, axis=0).astype(BF16)
    new_key_ref[...] = new_key
    key_rows_ref[...] = dot(back, new_key).astype(BF16)


def rank_kernel(total, capacity, *refs):
    rows, factors_ref, out_ref = refs[:total], refs[total], refs[total + 1]
    stacked = jnp.concatenate([ref[...] for ref in rows], axis=0)
    product = dot(stacked, factors_ref[...])
    out_ref[...] = jnp.concatenate(
        [product[2 * capacity * s : 2 * capacity * s + capacity] for s in range(total)], axis=0
    )


def query_kernel(total, capacity, sums, *refs):
    rows = refs[:total]
    partials = refs[total : total + sums]
    factors_ref, cosine_ref, sine_ref = refs[total + sums : total + sums + 3]
    outs = refs[total + sums + 3 :]
    slot_total = total * capacity
    level = [ref[...] for ref in partials]
    while len(level) > 1:
        level = [level[i] + level[i + 1] for i in range(0, len(level), 2)]
    rank = level[0].astype(BF16).astype(F32)
    lanes = lax.broadcasted_iota(jnp.int32, rank.shape, 1)
    split = jnp.concatenate(
        [jnp.where(lanes < ADAPTER_RANK, rank, 0.0), jnp.where(lanes < ADAPTER_RANK, 0.0, rank)],
        axis=0,
    ).astype(BF16)
    correction = (dot(split, factors_ref[...]) * ADAPTER_SCALE).astype(BF16).astype(F32)
    base = jnp.concatenate([ref[...].astype(F32)[capacity:] for ref in rows], axis=0)
    query = turn(base + correction[:slot_total], cosine_ref[0:1, :], sine_ref[0:1, :])
    for s in range(total):
        back = (total - s) % total
        first = slot_total + back * capacity
        outs[s][...] = jnp.concatenate(
            [query, correction[first : first + capacity]], axis=0
        ).astype(BF16)


def prefix_kernel(total, capacity, meta_ref, cache_ref, *refs):
    received, outs = refs[:total], refs[total : 2 * total]
    queries_ref, mixed_ref = refs[2 * total :]
    slot_total = total * capacity
    blocks, _, tokens, width = cache_ref.shape
    heads = width // HEAD_SIZE
    for s in range(total):
        queries_ref[s * slot_total : (s + 1) * slot_total, :] = received[s][0:slot_total, :]
    lanes = lax.broadcasted_iota(jnp.int32, (slot_total, HEAD_SIZE), 1)
    for b in range(blocks):
        source = meta_ref[slot_total + b]
        valid = meta_ref[slot_total + blocks + b]
        query = queries_ref[pl.ds(pl.multiple_of(source * slot_total, slot_total), slot_total), :]
        stats = jnp.zeros((slot_total, HEAD_SIZE), F32)
        for h in range(heads):
            part = slice(h * HEAD_SIZE, (h + 1) * HEAD_SIZE)
            scores = lax.dot_general(
                query[:, part],
                cache_ref[b, 0, :, part],
                (((1,), (1,)), ((), ())),
                preferred_element_type=F32,
            ) * HEAD_SIZE ** (-0.5)
            peak = jnp.max(scores, axis=1, keepdims=True)
            weights = jnp.exp(scores - peak)
            sums = jnp.sum(weights, axis=1, keepdims=True)
            stats = jnp.where(lanes == h, peak, stats)
            stats = jnp.where(lanes == heads + h, sums, stats)
            mixed_ref[b, :, part] = dot(weights.astype(BF16), cache_ref[b, 1, :, part])
        stats = jnp.where(jnp.logical_and(valid == 0, lanes < heads), NEG_FILL, stats)
        high = stats.astype(BF16).astype(F32)
        rest = stats - high
        middle = rest.astype(BF16).astype(F32)
        low = rest - middle
        mixed_ref[b, :, width:] = (
            high + pltpu.roll(middle, 2 * heads, 1) + pltpu.roll(low, 4 * heads, 1)
        )
        for s in range(total):
            group = host_offset(host_offset(-source, total) - s, total)
            outs[s][b] = mixed_ref[
                b, pl.ds(pl.multiple_of(group * capacity, capacity), capacity), :
            ].astype(BF16)


def head_ones(width, transposed):
    heads = width // HEAD_SIZE
    if transposed:
        rows = lax.broadcasted_iota(jnp.int32, (HEAD_SIZE, width), 0)
        features = lax.broadcasted_iota(jnp.int32, (HEAD_SIZE, width), 1)
    else:
        rows = lax.broadcasted_iota(jnp.int32, (width, HEAD_SIZE), 1)
        features = lax.broadcasted_iota(jnp.int32, (width, HEAD_SIZE), 0)
    inside = jnp.logical_and(features >= rows * HEAD_SIZE, features < (rows + 1) * HEAD_SIZE)
    return jnp.where(inside, 1.0, 0.0).astype(BF16)


def head_sums(products, ones):
    high = products.astype(BF16)
    low = (products - high.astype(F32)).astype(BF16)
    return dot(high, ones) + dot(low, ones)


def own_kernel(total, capacity, meta_ref, cache_ref, new_key_ref, packed_value_ref, unpack_ref, *refs):
    received = refs[:total]
    value_rows_ref, mixed_ref, peak_ref, sums_ref, product_ref = refs[total:]
    slot_total = total * capacity
    suffix = cache_ref.shape[2]
    width = cache_ref.shape[3]
    ones = head_ones(width, False)
    spread = head_ones(width, True)
    queries, corrections = [], []
    for r in range(total):
        full = received[(total - r) % total][...].astype(F32)
        queries.append(full[r * capacity : (r + 1) * capacity])
        corrections.append(full[slot_total : slot_total + capacity])
    query = jnp.concatenate(queries, axis=0)
    new_value = (packed_value_ref[...].astype(F32) + jnp.concatenate(corrections, axis=0)).astype(
        BF16
    )
    value_rows_ref[...] = dot(unpack_ref[...], new_value).astype(BF16)
    for s in range(slot_total):
        keys = cache_ref[meta_ref[s], 0].astype(F32)
        product_ref[s * suffix : (s + 1) * suffix, :] = keys * query[s : s + 1, :]
    scale = HEAD_SIZE ** (-0.5)
    scores = (head_sums(product_ref[...], ones) * scale).reshape(slot_total, suffix, HEAD_SIZE)
    new_scores = head_sums(new_key_ref[...].astype(F32) * query, ones) * scale
    peak = jnp.maximum(jnp.max(scores, axis=1), new_scores)
    weights = jnp.exp(scores - peak[:, None, :])
    new_weights = jnp.exp(new_scores - peak)
    peak_ref[...] = peak
    sums_ref[...] = jnp.sum(weights, axis=1) + new_weights
    product_ref[...] = dot(weights.reshape(slot_total * suffix, HEAD_SIZE).astype(BF16), spread)
    mixed_ref[...] = dot(new_weights.astype(BF16), spread) * new_value.astype(F32)
    for s in range(slot_total):
        values = cache_ref[meta_ref[s], 1].astype(F32)
        mixed_ref[s : s + 1, :] += jnp.sum(
            product_ref[s * suffix : (s + 1) * suffix, :] * values, axis=0, keepdims=True
        )


def combine_kernel(total, capacity, meta_ref, unpack_ref, mixed_ref, peak_ref, sums_ref, *refs):
    received, out_ref, parts_ref = refs[:total], refs[total], refs[total + 1]
    slot_total = total * capacity
    blocks = received[0].shape[0]
    width = mixed_ref.shape[1]
    heads = width // HEAD_SIZE
    for s in range(total):
        parts_ref[s * blocks : (s + 1) * blocks] = received[s][...]
    results = []
    for r in range(total):
        rows = slice(r * capacity, (r + 1) * capacity)
        overall = peak_ref[rows, :]
        pieces = []
        for j in range(PBLK):
            place = meta_ref[slot_total + 2 * blocks + r * PBLK + j]
            coded = parts_ref[place, :, width:].astype(F32)
            stats = (
                coded
                + pltpu.roll(coded, HEAD_SIZE - 2 * heads, 1)
                + pltpu.roll(coded, HEAD_SIZE - 4 * heads, 1)
            )
            pieces.append((place, stats, pltpu.roll(stats, HEAD_SIZE - heads, 1)))
            overall = jnp.maximum(overall, stats)
        own_factor = jnp.exp(peak_ref[rows, :] - overall)
        denominator = sums_ref[rows, :] * own_factor
        factors = []
        for place, top, sums in pieces:
            factor = jnp.exp(top - overall)
            factors.append(factor)
            denominator = denominator + sums * factor
        columns = []
        for h in range(heads):
            part = slice(h * HEAD_SIZE, (h + 1) * HEAD_SIZE)
            numerator = mixed_ref[rows, part] * own_factor[:, h : h + 1]
            for (place, _, _), factor in zip(pieces, factors):
                numerator = numerator + parts_ref[place, :, part].astype(F32) * factor[:, h : h + 1]
            columns.append(numerator / denominator[:, h : h + 1])
        results.append(jnp.concatenate(columns, axis=1))
    attended = jnp.concatenate(results, axis=0).astype(BF16)
    out_ref[...] = dot(unpack_ref[...], attended).astype(BF16)


def exchange(arrays):
    total = len(arrays)
    received = [arrays[0]]
    for s in range(1, total):
        ring = [(i, (i + s) % total) for i in range(total)]
        received.append(lax.ppermute(arrays[s], "hosts", ring))
    return received


def direct_body(
    hidden,
    base_query_projection,
    base_key_projection,
    base_value_projection,
    adapter_input_factors,
    adapter_output_factors,
    statement_prefix_cache,
    generated_token_cache,
    attempt_theorem_index,
    host_live_count,
    adapter_pool_row,
    prefix_pool_row,
    prefix_block_count,
):
    total = lax.axis_size("hosts")
    shares = lax.axis_size("mp")
    attempts, width = hidden.shape
    capacity = attempts // total
    slot_total = total * capacity
    blocks = statement_prefix_cache.shape[0]
    suffix = generated_token_cache.shape[2]
    input_factors = adapter_input_factors[0]
    output_factors = adapter_output_factors.reshape(2 * ADAPTER_RANK, width)
    taken = pltpu.SMEM((total,), jnp.int32)

    sent = pl.pallas_call(
        lambda *refs: send_kernel(total, capacity, *refs),
        out_shape=[shape_of(2 * capacity, width)] * total,
        in_specs=[SMEM] * 3 + [VMEM] * 2,
        out_specs=[VMEM] * total,
        scratch_shapes=[taken],
        name="send_rows",
        compiler_params=GRANT,
    )(attempt_theorem_index, host_live_count, adapter_pool_row, hidden, base_query_projection)
    rows = exchange(sent)

    me = lax.axis_index("hosts")
    owners = (me + jnp.arange(total, dtype=jnp.int32)) % total
    counts = jnp.sum(
        jnp.where(
            owners[:, None] == adapter_pool_row[None, :], prefix_block_count[None, :], 0
        ),
        axis=1,
    )
    position = (BLK * counts + suffix).astype(F32)
    frequency = ROPE_BASE ** (
        -(jnp.arange(HEAD_SIZE // 2, dtype=F32) * (2.0 / HEAD_SIZE))
    )
    angles = position[:, None] * frequency
    cosine = jnp.cos(angles)
    sine = jnp.sin(angles)
    cosine = jnp.concatenate([cosine, cosine], axis=1)
    sine = jnp.concatenate([-sine, sine], axis=1)

    key_rows, new_key, packed_value, unpack, meta = pl.pallas_call(
        lambda *refs: table_kernel(total, capacity, *refs),
        out_shape=[
            shape_of(attempts, width),
            shape_of(slot_total, width),
            shape_of(slot_total, width),
            shape_of(attempts, slot_total),
            shape_of(slot_total + 2 * blocks + total * PBLK + 1, kind=jnp.int32),
        ],
        in_specs=[SMEM] * 5 + [VMEM] * 4,
        out_specs=[VMEM] * 4 + [SMEM],
        scratch_shapes=[taken],
        name="slot_tables",
        compiler_params=GRANT,
    )(
        attempt_theorem_index,
        host_live_count,
        adapter_pool_row,
        prefix_pool_row,
        prefix_block_count,
        base_key_projection,
        base_value_projection,
        cosine,
        sine,
    )

    partial = pl.pallas_call(
        lambda *refs: rank_kernel(total, capacity, *refs),
        out_shape=shape_of(slot_total, 2 * ADAPTER_RANK, kind=F32),
        in_specs=[VMEM] * (total + 1),
        out_specs=VMEM,
        name="rank_rows",
        compiler_params=GRANT,
    )(*rows, input_factors)
    partials = [partial]
    for s in range(1, shares):
        partials.append(lax.ppermute(partial, "mp", [(i, i ^ s) for i in range(shares)]))

    answers = pl.pallas_call(
        lambda *refs: query_kernel(total, capacity, shares, *refs),
        out_shape=[shape_of(slot_total + capacity, width)] * total,
        in_specs=[VMEM] * (total + shares + 3),
        out_specs=[VMEM] * total,
        name="query_rows",
        compiler_params=GRANT,
    )(*rows, *partials, output_factors, cosine, sine)
    queries = exchange(answers)

    replies = pl.pallas_call(
        lambda *refs: prefix_kernel(total, capacity, *refs),
        out_shape=[shape_of(blocks, capacity, width + HEAD_SIZE)] * total,
        in_specs=[SMEM] + [VMEM] * (total + 1),
        out_specs=[VMEM] * total,
        scratch_shapes=[
            pltpu.VMEM((total * slot_total, width), BF16),
            pltpu.VMEM((blocks, slot_total, width + HEAD_SIZE), F32),
        ],
        name="prefix_attention",
        compiler_params=GRANT,
    )(meta, statement_prefix_cache, *queries)
    partial_rows = exchange(replies)

    value_rows, mixed, peak, sums = pl.pallas_call(
        lambda *refs: own_kernel(total, capacity, *refs),
        out_shape=[
            shape_of(attempts, width),
            shape_of(slot_total, width, kind=F32),
            shape_of(slot_total, HEAD_SIZE, kind=F32),
            shape_of(slot_total, HEAD_SIZE, kind=F32),
        ],
        in_specs=[SMEM] + [VMEM] * (total + 4),
        out_specs=[VMEM] * 4,
        scratch_shapes=[pltpu.VMEM((slot_total * suffix, width), F32)],
        name="own_attention",
        compiler_params=GRANT,
    )(meta, generated_token_cache, new_key, packed_value, unpack, *queries)

    attended = pl.pallas_call(
        lambda *refs: combine_kernel(total, capacity, *refs),
        out_shape=shape_of(attempts, width),
        in_specs=[SMEM] + [VMEM] * (total + 4),
        out_specs=VMEM,
        scratch_shapes=[pltpu.VMEM((total * blocks, capacity, width + HEAD_SIZE), BF16)],
        name="combine",
        compiler_params=GRANT,
    )(meta, unpack, mixed, peak, sums, *partial_rows)
    return attended, key_rows, value_rows


def body(*arguments):
    total = lax.axis_size("hosts")
    shares = lax.axis_size("mp")
    attempts, width = arguments[0].shape
    theorems = arguments[10].shape[0]
    blocks = arguments[6].shape[0]
    suffix = arguments[7].shape[2]
    direct = (
        total <= 8
        and shares & (shares - 1) == 0
        and arguments[4].shape[0] == 1
        and theorems == total
        and blocks * total == theorems * PBLK
        and attempts == 8 * total
        and 2 * total * 8 <= 128
        and suffix == 8
        and 6 * (width // HEAD_SIZE) <= HEAD_SIZE
    )
    return direct_body(*arguments) if direct else routed_body(*arguments)


def solution(mesh):
    placed = (
        P(("groups", "hosts"), "mp"),
        P(("groups", "hosts"), "mp"),
        P(("groups", "hosts"), "mp"),
        P(("groups", "hosts"), "mp"),
        P(("groups", "hosts"), "mp", None),
        P(("groups", "hosts"), None, None, "mp"),
        P(("groups", "hosts"), None, None, "mp"),
        P(("groups", "hosts"), None, None, "mp"),
        P(("groups", "hosts")),
        P(("groups", "hosts")),
        P("groups"),
        P("groups", None),
        P("groups"),
    )
    return jax.shard_map(
        body,
        mesh=mesh,
        in_specs=placed,
        out_specs=(
            P(("groups", "hosts"), "mp"),
            P(("groups", "hosts"), "mp"),
            P(("groups", "hosts"), "mp"),
        ),
        check_vma=False,
    )
```
